256 devices in a mesh: dom: 32 (over y, z_hi, x), cls: 8 (over z_lo, core).
Axes of the slice: x: 4, y: 4, z: 8 (z_hi: 2, z_lo: 4; z = z_hi * 4 + z_lo), core: 2. Of those that a mesh axis runs over, the one named last changes fastest.
Arguments:
- spectra: bfloat16 [32768, 2, 16512], P('dom', None, 'cls'), may hold values from -6 to 6
- classes: int32 [32768], P('dom'), may hold values from 0 to 63
- halves: int32 [32768], P('dom'), may hold values from 0 to 1
- groups: int32 [32768], P('dom'), may hold values from 0 to 15
- cycles: int32 [16512], P('dom'), may hold values from 0 to 127
- ctf_table: bfloat16 [16, 16512], replicated, may hold values from -1 to 1
- noise: float32 [128], replicated, may hold values from 0.5 to 8
Outputs:
- averages: bfloat16 [64, 2, 16512], replicated
The draws below stay inside these ranges and needn't reach their ends.
All inputs are finite; a program needn't handle non-finite values.
Results may differ from the reference program's by a relative error of at most 0.0067.
Values may be sent and summed in bfloat16 or wider, within the bound.
A program may use at most 64 MiB of HBM per device.

```python
import math
import jax
import jax.numpy as jnp
import numpy as np
from jax import lax

NPIX = 16512
K = 64
NRING = 128
G = 16
PARTICLES = 32768


def place_ends(result, key, smallest, largest):
    longest = result.shape.index(max(result.shape))
    spots = []
    for shift in (0, 1):
        where = [jax.random.randint(jax.random.fold_in(key, axis), (), 0, length) for axis, length in enumerate(result.shape)]
        where[longest] = (where[longest] + shift) % result.shape[longest]
        spots.append(tuple(where))
    return result.at[spots[0]].set(smallest).at[spots[1]].set(largest)


def steps_of(rng, shape, cuts, least, high):
    loudness, own = 1.0, jax.random.fold_in(rng, 6)
    for position, shards_of in cuts:
        heights = jnp.exp(jax.random.uniform(jax.random.fold_in(own, position), (shards_of,), jnp.float32, least / len(cuts), high / len(cuts)))
        loudness = loudness * jnp.repeat(heights, shape[position] // shards_of).reshape([-1 if axis == position else 1 for axis in range(len(shape))])
    return loudness


def cumulative_ranks(number_of, skew):
    loads = [(1 << 20) // math.isqrt(grade ** skew) + 1 for grade in range(1, number_of + 1)]
    spread = 1 + sum(loads) // (1 << 30)
    return np.cumsum(np.array([max(1, weight // spread) for weight in loads]))


def ranked(stream_key, dims, count, slope):
    listing = cumulative_ranks(count, slope)
    pick = jax.random.randint(jax.random.fold_in(stream_key, 1), dims, 0, int(listing[count - 1]))
    standing = jnp.searchsorted(jnp.asarray(listing, jnp.int32), pick, side="right")
    return jax.random.permutation(jax.random.fold_in(stream_key, 2), count)[standing].astype(jnp.int32)


def centred(key, shape, width, most, shards=(), held_as=jnp.bfloat16):
    values = jax.random.normal(key, shape, jnp.float32) * width
    if len(shards) > 0:
        values = steps_of(key, shape, shards, -0.22, 0.18) * values
    return jnp.clip(values, min=-most, max=most).astype(held_as)


def setup_inputs(seed: int = 0) -> dict:
    seeds = jax.random.split(jax.random.key(seed), 8)
    return {
        "spectra": centred(seeds[0], (PARTICLES, 2, NPIX), 1.0, 6.0, ((0, 32), (2, 8))),
        "classes": place_ends(ranked(seeds[1], (PARTICLES,), K, 2), jax.random.fold_in(seeds[1], 3), 0, K - 1).astype(jnp.int32),
        "halves": place_ends(jax.random.randint(seeds[2], (PARTICLES,), 0, 2), jax.random.fold_in(seeds[2], 1), 0, 1).astype(jnp.int32),
        "groups": place_ends(jax.random.randint(seeds[3], (PARTICLES,), 0, G), jax.random.fold_in(seeds[3], 1), 0, G - 1).astype(jnp.int32),
        "cycles": place_ends(jax.random.randint(seeds[4], (NPIX,), 0, NRING), jax.random.fold_in(seeds[4], 1), 0, NRING - 1).astype(jnp.int32),
        "ctf_table": jnp.clip(jax.random.uniform(seeds[5], (G, NPIX), jnp.float32, -1.0, 1.0), -1.0, 1.0).astype(jnp.bfloat16),
        "noise": jnp.clip(jnp.exp(jax.random.uniform(seeds[6], (NRING,), jnp.float32, math.log(0.5), math.log(8.0))), 0.5, 8.0),
    }


RIDGE = 1.0
GAIN_FLOOR = 0.02
EPSILON = 1e-06

def reference(spectra, classes, halves, groups, cycles, ctf_table, noise):
    total_rows = spectra.shape[0]
    pixels = spectra.shape[2]
    depth = ctf_table.shape[0]
    cycle_total = noise.shape[0]
    block = math.gcd(total_rows, 1024)
    square_table = (ctf_table.astype(jnp.float32) ** 2).astype(jnp.bfloat16)
    highest = lax.Precision.HIGHEST

    def accumulate(carry, index):
        sums, wsum = carry
        begin = (index * block).astype(jnp.int32)
        spec_block = lax.dynamic_slice_in_dim(spectra, begin, block, 0)
        class_block = lax.dynamic_slice_in_dim(classes, begin, block, 0)
        half_block = lax.dynamic_slice_in_dim(halves, begin, block, 0)
        group_block = lax.dynamic_slice_in_dim(groups, begin, block, 0)
        group_hot = (group_block[:, None] == jnp.arange(depth, dtype=jnp.int32)[None, :]).astype(jnp.bfloat16)
        ctf = jnp.dot(group_hot, ctf_table, preferred_element_type=jnp.float32)
        weighted = (ctf[:, None, :] * spec_block.astype(jnp.float32)).astype(jnp.bfloat16)
        squares = jnp.dot(group_hot, square_table, preferred_element_type=jnp.float32).astype(jnp.bfloat16)
        labels = half_block * K + class_block
        class_hot = (labels[:, None] == jnp.arange(2 * K, dtype=jnp.int32)[None, :]).astype(jnp.float32)
        sums = sums + jnp.einsum('pm,pcn->mcn', class_hot, weighted.astype(jnp.float32), precision=highest)
        wsum = wsum + jnp.dot(class_hot.T, squares.astype(jnp.float32), precision=highest, preferred_element_type=jnp.float32)
        return ((sums, wsum), None)
    start_sums = jnp.zeros((2 * K, 2, pixels), jnp.float32)
    start_wsum = jnp.zeros((2 * K, pixels), jnp.float32)
    (sums, wsum), _ = lax.scan(accumulate, (start_sums, start_wsum), jnp.arange(total_rows // block, dtype=jnp.int32))
    sums = sums.reshape(2, K, 2, pixels)
    wsum = wsum.reshape(2, K, pixels)
    halfavg = sums / (wsum[:, :, None, :] + RIDGE)
    cycle_hot = (cycles[:, None] == jnp.arange(cycle_total, dtype=jnp.int32)[None, :]).astype(jnp.float32)
    cross = jnp.dot(lax.optimization_barrier(jnp.sum(halfavg[0] * halfavg[1], axis=1)), cycle_hot, precision=highest)
    power_zero = jnp.dot(lax.optimization_barrier(jnp.sum(halfavg[0] * halfavg[0], axis=1)), cycle_hot, precision=highest)
    power_one = jnp.dot(lax.optimization_barrier(jnp.sum(halfavg[1] * halfavg[1], axis=1)), cycle_hot, precision=highest)
    correlation = cross / jnp.sqrt((power_zero + noise[None, :]) * (power_one + noise[None, :]))
    gain = jnp.maximum(correlation, GAIN_FLOOR)
    merged = (sums[0] + sums[1]) / (wsum[0] + wsum[1] + RIDGE)[:, None, :]
    gain_pixels = jnp.dot(gain, cycle_hot.T, precision=highest)
    filtered = merged * gain_pixels[:, None, :]
    power = lax.optimization_barrier(jnp.sum(filtered * filtered, axis=(1, 2))) / (2.0 * pixels)
    return (filtered / jnp.sqrt(power + EPSILON)[:, None, None]).astype(jnp.bfloat16)
```

```python
import jax
import jax.numpy as jnp
from jax import lax
from jax.sharding import PartitionSpec as P

K = 64
RIDGE = 1.0
GAIN_FLOOR = 0.02
EPSILON = 1e-06
STEP = 32


def local(spectra, classes, halves, groups, cycles, ctf_table, noise):
    highest = lax.Precision.HIGHEST
    local_particles, channels, local_pixels = spectra.shape
    depth = ctf_table.shape[0]
    pixels = ctf_table.shape[1]
    cycle_total = noise.shape[0]
    dom_count = lax.axis_size("dom")
    owned_rows = 2 * K // dom_count
    width = channels * local_pixels
    pixel_begin = lax.axis_index("cls") * local_pixels
    every_cycle = lax.all_gather(cycles, "dom", axis=0, tiled=True)
    ctf_local = lax.dynamic_slice_in_dim(ctf_table, pixel_begin, local_pixels, 1)
    group_hot = (groups[:, None] == jnp.arange(depth, dtype=jnp.int32)[None, :]).astype(
        jnp.bfloat16
    )
    labels = classes * 2 + halves
    class_hot = (labels[:, None] == jnp.arange(2 * K, dtype=jnp.int32)[None, :]).astype(
        jnp.bfloat16
    )
    ctf = jnp.dot(group_hot, ctf_local, preferred_element_type=jnp.float32)
    weighted = (ctf[:, None, :] * spectra).astype(jnp.bfloat16)
    partial_sums = jnp.einsum("pm,pcn->mcn", class_hot, weighted, preferred_element_type=jnp.float32)
    counts = jnp.einsum("pm,pg->mg", class_hot, group_hot, preferred_element_type=jnp.float32)
    high = jnp.floor(counts / STEP)
    low = counts - high * STEP
    message = jnp.concatenate(
        [partial_sums.reshape(2 * K, width), high, low], axis=1
    ).astype(jnp.bfloat16)
    received = lax.all_to_all(
        message.reshape(dom_count, owned_rows, -1), "dom", split_axis=0, concat_axis=0, tiled=True
    )
    total = jnp.sum(received.astype(jnp.float32), axis=0)
    sums = total[:, :width].reshape(owned_rows // 2, 2, channels, local_pixels)
    count_total = total[:, width : width + depth] * STEP + total[:, width + depth :]
    square_local = (ctf_local.astype(jnp.float32) ** 2).astype(jnp.bfloat16).astype(jnp.float32)
    wsum = jnp.dot(count_total, square_local, precision=highest).reshape(
        owned_rows // 2, 2, local_pixels
    )
    halfavg = sums / (wsum[:, :, None, :] + RIDGE)
    first_half = halfavg[:, 0]
    second_half = halfavg[:, 1]
    merged = (sums[:, 0] + sums[:, 1]) / (wsum[:, 0] + wsum[:, 1] + RIDGE)[:, None, :]
    cross = jnp.sum(first_half * second_half, axis=1)
    power_zero = jnp.sum(first_half * first_half, axis=1)
    power_one = jnp.sum(second_half * second_half, axis=1)
    statistics = jnp.stack([cross, power_zero, power_one], axis=1)
    cycle_local = lax.dynamic_slice_in_dim(every_cycle, pixel_begin, local_pixels, 0)
    cycle_hot = (cycle_local[:, None] == jnp.arange(cycle_total, dtype=jnp.int32)[None, :]).astype(
        jnp.float32
    )
    cycle_sums = jnp.einsum("ksn,nr->ksr", statistics, cycle_hot, precision=highest)
    merged_power = jnp.sum(merged * merged, axis=1)
    merged_sums = jnp.einsum("kn,nr->kr", merged_power, cycle_hot, precision=highest)
    cycle_totals = lax.psum(jnp.concatenate([cycle_sums, merged_sums[:, None]], axis=1), "cls")
    correlation = cycle_totals[:, 0] / jnp.sqrt(
        (cycle_totals[:, 1] + noise[None, :]) * (cycle_totals[:, 2] + noise[None, :])
    )
    gain = jnp.maximum(correlation, GAIN_FLOOR)
    power_mean = jnp.sum(gain * gain * cycle_totals[:, 3], axis=1) / (2.0 * pixels)
    scale = gain / jnp.sqrt(power_mean + EPSILON)[:, None]
    scale_pixels = jnp.dot(scale, cycle_hot.T, precision=highest)
    normalized = (merged * scale_pixels[:, None, :]).astype(jnp.bfloat16)
    gathered = lax.all_gather(normalized, ("dom", "cls"), axis=0, tiled=False)
    gathered = gathered.reshape(dom_count, -1, owned_rows // 2, channels, local_pixels)
    return jnp.transpose(gathered, (0, 2, 3, 1, 4)).reshape(K, channels, pixels)


def solution(mesh):
    placed = (P("dom", None, "cls"), P("dom"), P("dom"), P("dom"), P("dom"), P(), P())
    return jax.shard_map(local, mesh=mesh, in_specs=placed, out_specs=P(), check_vma=False)
```

```python
import functools

import jax
import jax.numpy as jnp
from jax import lax
from jax.experimental import pallas as pl
from jax.experimental.pallas import tpu as pltpu
from jax.sharding import PartitionSpec as P

K = 64
RIDGE = 1.0
GAIN_FLOOR = 0.02
EPSILON = 1e-06
STEP = 32
NY, NZ, NX, NC = 4, 2, 4, 2
MESH = pl.DeviceIdType.MESH


def gather_kernel(unit_ref, out_ref, own_sem, z_send, z_recv, x_send, x_recv, y_send, y_recv, c_send, c_recv):
    dom = lax.axis_index("dom")
    cls = lax.axis_index("cls")
    y = lax.div(dom, NZ * NX)
    z = lax.rem(lax.div(dom, NX), NZ)
    x = lax.rem(dom, NX)
    core = lax.rem(cls, NC)
    other = 1 - z

    def at(yy, zz, xx):
        return ((yy * NZ + zz) * NX + xx, cls)

    partner = (dom, cls + 1 - 2 * core)
    z_peer = at(y, other, x)
    x_peers = [at(y, z, lax.rem(x + j, NX)) for j in range(1, NX)]
    y_peers = [at(lax.rem(y + j, NY), z, x) for j in range(1, NY)]
    x_from = [lax.rem(x + NX - j, NX) for j in range(1, NX)]
    y_from = [lax.rem(y + NY - j, NY) for j in range(1, NY)]

    barrier = pltpu.get_barrier_semaphore()
    everyone = [partner, z_peer] + x_peers + y_peers
    for peer in everyone:
        pl.semaphore_signal(barrier, inc=1, device_id=peer, device_id_type=MESH)
    pl.semaphore_wait(barrier, len(everyone))

    def send(src, dst, send_sem, recv_sem, peer):
        copy = pltpu.make_async_remote_copy(
            src_ref=src, dst_ref=dst, send_sem=send_sem, recv_sem=recv_sem,
            device_id=peer, device_id_type=MESH,
        )
        copy.start()
        return copy

    mine = out_ref.at[y, z, x, core]
    own = pltpu.make_async_copy(unit_ref, mine, own_sem)
    own.start()
    to_z = send(unit_ref, mine, z_send, z_recv, z_peer)
    first_x = [
        send(unit_ref, mine, x_send.at[j], x_recv.at[j], x_peers[j]) for j in range(NX - 1)
    ]
    to_z.wait_recv()
    cross = out_ref.at[y, other, x, core]
    first_y = [send(cross, cross, y_send.at[j], y_recv.at[j], y_peers[j]) for j in range(NY - 1)]
    own.wait()
    for copy in first_x:
        copy.wait_recv()
    row = out_ref.at[y, z, :, core]
    second_y = [
        send(row, row, y_send.at[NY - 1 + j], y_recv.at[NY - 1 + j], y_peers[j])
        for j in range(NY - 1)
    ]
    to_core = [send(row, row, c_send.at[0], c_recv.at[0], partner)]
    for copy in first_y:
        copy.wait_recv()
    column = out_ref.at[:, other, x, core]
    second_x = [
        send(column, column, x_send.at[NX - 1 + j], x_recv.at[NX - 1 + j], x_peers[j])
        for j in range(NX - 1)
    ]
    to_core.append(send(column, column, c_send.at[1], c_recv.at[1], partner))
    for j in range(NY - 1):
        second_y[j].wait_recv()
        far = out_ref.at[y_from[j], z, :, core]
        to_core.append(send(far, far, c_send.at[2 + j], c_recv.at[2 + j], partner))
    for j in range(NX - 1):
        second_x[j].wait_recv()
        far = out_ref.at[:, other, x_from[j], core]
        slot = 1 + NY + j
        to_core.append(send(far, far, c_send.at[slot], c_recv.at[slot], partner))
    for copy in to_core:
        copy.wait_recv()
    for copy in [to_z] + first_x + first_y + second_y + second_x + to_core:
        copy.wait_send()


def gather(unit):
    channels, pixels = unit.shape
    dma = pltpu.SemaphoreType.DMA
    out = pl.pallas_call(
        gather_kernel,
        out_shape=jax.ShapeDtypeStruct((NY, NZ, NX, NC, channels, pixels), unit.dtype),
        in_specs=[pl.BlockSpec(memory_space=pl.ANY)],
        out_specs=pl.BlockSpec(memory_space=pl.ANY),
        scratch_shapes=[
            dma,
            dma,
            dma,
            dma((2 * (NX - 1),)),
            dma((2 * (NX - 1),)),
            dma((2 * (NY - 1),)),
            dma((2 * (NY - 1),)),
            dma((NX + NY,)),
            dma((NX + NY,)),
        ],
        compiler_params=pltpu.CompilerParams(collective_id=0, has_side_effects=True),
    )(unit)
    return out.reshape(NY * NZ * NX * NC, channels, pixels)


def split(value):
    parts = []
    for _ in range(3):
        part = lax.reduce_precision(value, 8, 7)
        parts.append(part.astype(jnp.bfloat16))
        value = value - part
    return jnp.concatenate(parts, axis=0)


def local(spectra, classes, halves, groups, cycles, ctf_table, noise):
    highest = lax.Precision.HIGHEST
    local_particles, channels, local_pixels = spectra.shape
    depth = ctf_table.shape[0]
    pixels = ctf_table.shape[1]
    cycle_total = noise.shape[0]
    dom_count = lax.axis_size("dom")
    cls_count = lax.axis_size("cls")
    owned_rows = 2 * K // dom_count
    width = channels * local_pixels
    pixel_begin = lax.axis_index("cls") * local_pixels
    ctf_local = lax.dynamic_slice_in_dim(ctf_table, pixel_begin, local_pixels, 1)
    group_hot = (groups[:, None] == jnp.arange(depth, dtype=jnp.int32)[None, :]).astype(
        jnp.bfloat16
    )
    labels = classes * 2 + halves
    class_hot = (labels[:, None] == jnp.arange(2 * K, dtype=jnp.int32)[None, :]).astype(
        jnp.bfloat16
    )
    ctf = jnp.dot(group_hot, ctf_local, preferred_element_type=jnp.float32)
    weighted = (ctf[:, None, :] * spectra).astype(jnp.bfloat16)
    partial_sums = jnp.einsum("pm,pcn->mcn", class_hot, weighted, preferred_element_type=jnp.float32)
    counts = jnp.einsum("pm,pg->mg", class_hot, group_hot, preferred_element_type=jnp.float32)
    high = jnp.floor(counts / STEP)
    low = counts - high * STEP
    shared = cycles.astype(jnp.float32).reshape(owned_rows, -1)
    shared = jnp.tile(shared, (dom_count, 1))
    message = jnp.concatenate(
        [partial_sums.reshape(2 * K, width), high, low, shared], axis=1
    ).astype(jnp.bfloat16)
    received = lax.all_to_all(
        message.reshape(dom_count, owned_rows, -1), "dom", split_axis=0, concat_axis=0, tiled=True
    )
    every_cycle = received[:, :, width + 2 * depth :].astype(jnp.int32).reshape(pixels)
    total = jnp.sum(received[:, :, : width + 2 * depth].astype(jnp.float32), axis=0)
    count_total = total[:, width : width + depth] * STEP + total[:, width + depth :]
    outgoing = total[:, :width].reshape(1, NC, 2 * channels, local_pixels)
    outgoing = jnp.tile(outgoing, (cls_count // NC, 1, 1, 1)).reshape(
        cls_count, 2 * channels, local_pixels
    )
    incoming = lax.all_to_all(outgoing, "cls", split_axis=0, concat_axis=0, tiled=True)
    sums = jnp.transpose(incoming, (1, 0, 2)).reshape(2, channels, pixels)
    core = lax.rem(lax.axis_index("cls"), NC)
    count_mine = lax.dynamic_slice_in_dim(count_total, core * 2, 2, 0)
    square_table = (ctf_table.astype(jnp.float32) ** 2).astype(jnp.bfloat16)
    parts = jnp.dot(split(count_mine), square_table, preferred_element_type=jnp.float32)
    wsum = parts.reshape(3, 2, pixels).sum(axis=0)
    halfavg = sums / (wsum[:, None, :] + RIDGE)
    merged = (sums[0] + sums[1]) / (wsum[0] + wsum[1] + RIDGE)[None, :]
    statistics = jnp.stack(
        [
            jnp.sum(halfavg[0] * halfavg[1], axis=0),
            jnp.sum(halfavg[0] * halfavg[0], axis=0),
            jnp.sum(halfavg[1] * halfavg[1], axis=0),
            jnp.sum(merged * merged, axis=0),
        ],
        axis=0,
    )
    rings = jnp.arange(cycle_total, dtype=jnp.int32)
    cycle_hot = (rings[:, None] == every_cycle[None, :]).astype(jnp.bfloat16)
    totals = jnp.einsum("sn,rn->sr", split(statistics), cycle_hot, preferred_element_type=jnp.float32)
    totals = totals.reshape(3, 4, cycle_total).sum(axis=0)
    correlation = totals[0] / jnp.sqrt((totals[1] + noise) * (totals[2] + noise))
    gain = jnp.maximum(correlation, GAIN_FLOOR)
    power_mean = jnp.sum(gain * gain * totals[3]) / (2.0 * pixels)
    scale = (gain / jnp.sqrt(power_mean + EPSILON))[None, :]
    scale_pixels = jnp.sum(
        jnp.dot(split(scale), cycle_hot, preferred_element_type=jnp.float32), axis=0
    )
    return gather((merged * scale_pixels[None, :]).astype(jnp.bfloat16))


def solution(mesh):
    placed = (P("dom", None, "cls"), P("dom"), P("dom"), P("dom"), P("dom"), P(), P())
    return jax.shard_map(local, mesh=mesh, in_specs=placed, out_specs=P(), check_vma=False)
```

```python
import functools

import jax
import jax.numpy as jnp
from jax import lax
from jax.experimental import pallas as pl
from jax.experimental.pallas import tpu as pltpu
from jax.sharding import PartitionSpec as P

K = 64
RIDGE = 1.0
GAIN_FLOOR = 0.02
EPSILON = 1e-06
STEP = 16
LANES = 128
NY, NZ, NX, NC = 4, 2, 4, 2
MESH = pl.DeviceIdType.MESH


def gather_kernel(unit_ref, out_ref, own_sem, z_send, z_recv, x_send, x_recv, y_send, y_recv, c_send, c_recv):
    dom = lax.axis_index("dom")
    cls = lax.axis_index("cls")
    y = lax.div(dom, NZ * NX)
    z = lax.rem(lax.div(dom, NX), NZ)
    x = lax.rem(dom, NX)
    core = lax.rem(cls, NC)
    other = 1 - z

    def at(yy, zz, xx):
        return ((yy * NZ + zz) * NX + xx, cls)

    partner = (dom, cls + 1 - 2 * core)
    z_peer = at(y, other, x)
    x_peers = [at(y, z, lax.rem(x + j, NX)) for j in range(1, NX)]
    y_peers = [at(lax.rem(y + j, NY), z, x) for j in range(1, NY)]
    x_from = [lax.rem(x + NX - j, NX) for j in range(1, NX)]
    y_from = [lax.rem(y + NY - j, NY) for j in range(1, NY)]

    barrier = pltpu.get_barrier_semaphore()
    everyone = [partner, z_peer] + x_peers + y_peers
    for peer in everyone:
        pl.semaphore_signal(barrier, inc=1, device_id=peer, device_id_type=MESH)
    pl.semaphore_wait(barrier, len(everyone))

    def send(src, dst, send_sem, recv_sem, peer):
        copy = pltpu.make_async_remote_copy(
            src_ref=src, dst_ref=dst, send_sem=send_sem, recv_sem=recv_sem,
            device_id=peer, device_id_type=MESH,
        )
        copy.start()
        return copy

    mine = out_ref.at[y, z, x, core]
    own = pltpu.make_async_copy(unit_ref, mine, own_sem)
    own.start()
    to_z = send(unit_ref, mine, z_send, z_recv, z_peer)
    first_x = [
        send(unit_ref, mine, x_send.at[j], x_recv.at[j], x_peers[j]) for j in range(NX - 1)
    ]
    to_z.wait_recv()
    cross = out_ref.at[y, other, x, core]
    first_y = [send(cross, cross, y_send.at[j], y_recv.at[j], y_peers[j]) for j in range(NY - 1)]
    own.wait()
    for copy in first_x:
        copy.wait_recv()
    row = out_ref.at[y, z, :, core]
    second_y = [
        send(row, row, y_send.at[NY - 1 + j], y_recv.at[NY - 1 + j], y_peers[j])
        for j in range(NY - 1)
    ]
    to_core = [send(row, row, c_send.at[0], c_recv.at[0], partner)]
    for copy in first_y:
        copy.wait_recv()
    column = out_ref.at[:, other, x, core]
    second_x = [
        send(column, column, x_send.at[NX - 1 + j], x_recv.at[NX - 1 + j], x_peers[j])
        for j in range(NX - 1)
    ]
    to_core.append(send(column, column, c_send.at[1], c_recv.at[1], partner))
    for j in range(NY - 1):
        second_y[j].wait_recv()
        far = out_ref.at[y_from[j], z, :, core]
        to_core.append(send(far, far, c_send.at[2 + j], c_recv.at[2 + j], partner))
    for j in range(NX - 1):
        second_x[j].wait_recv()
        far = out_ref.at[:, other, x_from[j], core]
        slot = 1 + NY + j
        to_core.append(send(far, far, c_send.at[slot], c_recv.at[slot], partner))
    for copy in to_core:
        copy.wait_recv()
    for copy in [to_z] + first_x + first_y + second_y + second_x + to_core:
        copy.wait_send()


def gather(unit):
    channels, pixels = unit.shape
    dma = pltpu.SemaphoreType.DMA
    out = pl.pallas_call(
        gather_kernel,
        out_shape=jax.ShapeDtypeStruct((NY, NZ, NX, NC, channels, pixels), unit.dtype),
        in_specs=[pl.BlockSpec(memory_space=pl.ANY)],
        out_specs=pl.BlockSpec(memory_space=pl.ANY),
        scratch_shapes=[
            dma,
            dma,
            dma,
            dma((2 * (NX - 1),)),
            dma((2 * (NX - 1),)),
            dma((2 * (NY - 1),)),
            dma((2 * (NY - 1),)),
            dma((NX + NY,)),
            dma((NX + NY,)),
        ],
        compiler_params=pltpu.CompilerParams(
            collective_id=0, has_side_effects=True, vmem_limit_bytes=8 << 20
        ),
    )(unit)
    return out.reshape(NY * NZ * NX * NC, channels, pixels)


def reduce_kernel(
    message_ref, cycles_ref, out_ref, cycles_out_ref,
    got, staged, far,
    own_sem, plane_send, plane_recv, column_send, column_recv, cycle_send, cycle_recv,
):
    dom = lax.axis_index("dom")
    cls = lax.axis_index("cls")
    y = lax.div(dom, NZ * NX)
    z = lax.rem(lax.div(dom, NX), NZ)
    x = lax.rem(dom, NX)
    core = lax.rem(cls, NC)
    groups = far.shape[1]
    rows = far.shape[2]
    doms = NY * NZ * NX

    plane = []
    for dy in range(NY):
        for dx in range(NX):
            plane.append((lax.rem(y + dy, NY), lax.rem(x + dx, NX)))
    column = []
    for dz in range(NZ):
        for dc in range(groups):
            column.append((lax.rem(z + dz, NZ), lax.rem(cls + dc, groups)))
    others = [lax.rem(dom + step, doms) for step in range(1, doms)]

    barrier = pltpu.get_barrier_semaphore()
    greeted = [(there, cls) for there in others]
    for step, (zz, cc) in enumerate(column):
        if step % groups:
            greeted.append(((y * NZ + zz) * NX + x, cc))
    for peer in greeted:
        pl.semaphore_signal(barrier, inc=1, device_id=peer, device_id_type=MESH)
    pl.semaphore_wait(barrier, len(greeted))

    own = pltpu.make_async_copy(message_ref.at[y, :, x], got.at[0], own_sem.at[0])
    own.start()
    own_cycles = pltpu.make_async_copy(cycles_ref, cycles_out_ref.at[dom], own_sem.at[1])
    own_cycles.start()
    sends = []
    for step in range(1, NY * NX):
        yy, xx = plane[step]
        copy = pltpu.make_async_remote_copy(
            src_ref=message_ref.at[yy, :, xx], dst_ref=got.at[step],
            send_sem=plane_send.at[step], recv_sem=plane_recv.at[step],
            device_id=((yy * NZ + z) * NX + xx, cls), device_id_type=MESH,
        )
        copy.start()
        sends.append(copy)
    for there in others:
        pltpu.make_async_remote_copy(
            src_ref=cycles_ref, dst_ref=cycles_out_ref.at[dom],
            send_sem=cycle_send, recv_sem=cycle_recv,
            device_id=(there, cls), device_id_type=MESH,
        ).start()
    own.wait()
    for copy in sends:
        copy.wait_recv()
    for zz in range(NZ):
        total = got[0, zz].astype(jnp.float32)
        for step in range(1, NY * NX):
            total = total + got[step, zz].astype(jnp.float32)
        total = total.astype(jnp.bfloat16)
        for cc in range(NC):
            staged[zz, cc] = total[cc * rows : (cc + 1) * rows]
    kept = pltpu.make_async_copy(staged.at[z, core], far.at[z, cls], own_sem.at[2])
    kept.start()
    relays = []
    for step in range(1, NZ * groups):
        zz, cc = column[step]
        copy = pltpu.make_async_remote_copy(
            src_ref=staged.at[zz, lax.rem(cc, NC)], dst_ref=far.at[z, cls],
            send_sem=column_send.at[step], recv_sem=column_recv.at[step],
            device_id=((y * NZ + zz) * NX + x, cc), device_id_type=MESH,
        )
        copy.start()
        relays.append(copy)
    kept.wait()
    for copy in relays:
        copy.wait_recv()
    for cc in range(groups):
        out_ref[cc] = far[0, cc].astype(jnp.float32) + far[1, cc].astype(jnp.float32)
    own_cycles.wait()
    span = cycles_out_ref.at[pl.ds(0, doms - 1)]
    pltpu.make_async_copy(span, span, cycle_recv).wait()
    pltpu.make_async_copy(span, span, cycle_send).wait()
    for copy in sends + relays:
        copy.wait_send()


def reduce(message, cycles, groups):
    doms, rows, width = message.shape
    dma = pltpu.SemaphoreType.DMA
    half = rows // NC
    return pl.pallas_call(
        reduce_kernel,
        out_shape=(
            jax.ShapeDtypeStruct((groups, half, width), jnp.float32),
            jax.ShapeDtypeStruct((doms,) + cycles.shape, cycles.dtype),
        ),
        in_specs=[pl.BlockSpec(memory_space=pltpu.VMEM)] * 2,
        out_specs=(pl.BlockSpec(memory_space=pltpu.VMEM),) * 2,
        scratch_shapes=[
            pltpu.VMEM((NY * NX, NZ, rows, width), jnp.bfloat16),
            pltpu.VMEM((NZ, NC, half, width), jnp.bfloat16),
            pltpu.VMEM((NZ, groups, half, width), jnp.bfloat16),
            dma((3,)),
            dma((NY * NX,)),
            dma((NY * NX,)),
            dma((NZ * groups,)),
            dma((NZ * groups,)),
            dma,
            dma,
        ],
        compiler_params=pltpu.CompilerParams(
            collective_id=1, has_side_effects=True, vmem_limit_bytes=16 << 20
        ),
    )(message.reshape(NY, NZ, NX, rows, width), cycles)


def split(value):
    parts = []
    for _ in range(3):
        part = lax.reduce_precision(value, 8, 7)
        parts.append(part.astype(jnp.bfloat16))
        value = value - part
    return jnp.concatenate(parts, axis=0)


def local(spectra, classes, halves, groups, cycles, ctf_table, noise):
    local_particles, channels, local_pixels = spectra.shape
    depth = ctf_table.shape[0]
    pixels = ctf_table.shape[1]
    cycle_total = noise.shape[0]
    dom_count = lax.axis_size("dom")
    cls_count = lax.axis_size("cls")
    owned_rows = 2 * K // dom_count
    pixel_begin = lax.axis_index("cls") * local_pixels
    ctf_local = lax.dynamic_slice_in_dim(ctf_table, pixel_begin, local_pixels, 1)
    group_hot = (groups[:, None] == jnp.arange(depth, dtype=jnp.int32)[None, :]).astype(
        jnp.bfloat16
    )
    labels = classes * 2 + halves
    class_hot = (labels[:, None] == jnp.arange(2 * K, dtype=jnp.int32)[None, :]).astype(
        jnp.bfloat16
    )
    ctf = jnp.dot(group_hot, ctf_local, preferred_element_type=jnp.float32)
    weighted = (ctf[:, None, :] * spectra).astype(jnp.bfloat16)
    partial_sums = jnp.einsum("pm,pcn->mcn", class_hot, weighted, preferred_element_type=jnp.float32)
    counts = jnp.einsum("pm,pg->mg", class_hot, group_hot, preferred_element_type=jnp.float32)
    counts = counts.astype(jnp.int32)
    digits = jnp.concatenate(
        [counts % STEP, (counts // STEP) % STEP, counts // (STEP * STEP)], axis=1
    )
    spare = -(local_pixels + 3 * depth) % LANES + 3 * depth
    digits = jnp.pad(digits[:, None, :], ((0, 0), (0, channels - 1), (0, spare - 3 * depth)))
    message = jnp.concatenate(
        [partial_sums.astype(jnp.bfloat16), digits.astype(jnp.bfloat16)], axis=2
    )
    cycle_rows = -(-cycles.shape[0] // (8 * LANES)) * 8
    cycle_block = jnp.pad(cycles, (0, cycle_rows * LANES - cycles.shape[0]))
    incoming, every_cycle = reduce(
        message.reshape(dom_count, owned_rows * channels, local_pixels + spare),
        cycle_block.reshape(cycle_rows, LANES),
        cls_count,
    )
    every_cycle = every_cycle.reshape(dom_count, -1)[:, : cycles.shape[0]].reshape(pixels)
    sums = jnp.transpose(incoming[:, :, :local_pixels], (1, 0, 2)).reshape(2, channels, pixels)
    found = incoming[0, ::channels, local_pixels : local_pixels + 3 * depth].reshape(2, 3, depth)
    count_mine = found[:, 0] + STEP * found[:, 1] + (STEP * STEP) * found[:, 2]
    square_table = (ctf_table.astype(jnp.float32) ** 2).astype(jnp.bfloat16)
    parts = jnp.dot(split(count_mine), square_table, preferred_element_type=jnp.float32)
    wsum = parts.reshape(3, 2, pixels).sum(axis=0)
    halfavg = sums / (wsum[:, None, :] + RIDGE)
    merged = (sums[0] + sums[1]) / (wsum[0] + wsum[1] + RIDGE)[None, :]
    statistics = jnp.stack(
        [
            jnp.sum(halfavg[0] * halfavg[1], axis=0),
            jnp.sum(halfavg[0] * halfavg[0], axis=0),
            jnp.sum(halfavg[1] * halfavg[1], axis=0),
            jnp.sum(merged * merged, axis=0),
        ],
        axis=0,
    )
    rings = jnp.arange(cycle_total, dtype=jnp.int32)
    cycle_hot = (rings[:, None] == every_cycle[None, :]).astype(jnp.bfloat16)
    totals = jnp.einsum("sn,rn->sr", split(statistics), cycle_hot, preferred_element_type=jnp.float32)
    totals = totals.reshape(3, 4, cycle_total).sum(axis=0)
    correlation = totals[0] / jnp.sqrt((totals[1] + noise) * (totals[2] + noise))
    gain = jnp.maximum(correlation, GAIN_FLOOR)
    power_mean = jnp.sum(gain * gain * totals[3]) / (2.0 * pixels)
    scale = (gain / jnp.sqrt(power_mean + EPSILON))[None, :]
    scale_pixels = jnp.sum(
        jnp.dot(split(scale), cycle_hot, preferred_element_type=jnp.float32), axis=0
    )
    return gather((merged * scale_pixels[None, :]).astype(jnp.bfloat16))


def solution(mesh):
    placed = (P("dom", None, "cls"), P("dom"), P("dom"), P("dom"), P("dom"), P(), P())
    return jax.shard_map(local, mesh=mesh, in_specs=placed, out_specs=P(), check_vma=False)
```

```python
import functools

import jax
import jax.numpy as jnp
from jax import lax
from jax.experimental import pallas as pl
from jax.experimental.pallas import tpu as pltpu
from jax.sharding import PartitionSpec as P

K = 64
RIDGE = 1.0
GAIN_FLOOR = 0.02
EPSILON = 1e-06
STEP = 16
LANES = 128
NY, NZ, NX, NC = 4, 2, 4, 2
MESH = pl.DeviceIdType.MESH


def gather_kernel(unit_ref, out_ref, own_sem, z_send, z_recv, x_send, x_recv, y_send, y_recv, c_send, c_recv):
    dom = lax.axis_index("dom")
    cls = lax.axis_index("cls")
    y = lax.div(dom, NZ * NX)
    z = lax.rem(lax.div(dom, NX), NZ)
    x = lax.rem(dom, NX)
    core = lax.rem(cls, NC)
    other = 1 - z

    def at(yy, zz, xx):
        return ((yy * NZ + zz) * NX + xx, cls)

    partner = (dom, cls + 1 - 2 * core)
    z_peer = at(y, other, x)
    turn = 1 - 2 * core
    x_next, x_last = lax.rem(x + turn + NX, NX), lax.rem(x - turn + NX, NX)
    y_next, y_last = lax.rem(y + turn + NY, NY), lax.rem(y - turn + NY, NY)
    x_far, y_far = lax.rem(x + 2, NX), lax.rem(y + 2, NY)
    x_peers = [at(y, z, x_next), at(y, z, x_last)]
    y_peers = [at(y_next, z, x), at(y_last, z, x)]

    barrier = pltpu.get_barrier_semaphore()
    everyone = [partner, z_peer] + x_peers + y_peers
    for peer in everyone:
        pl.semaphore_signal(barrier, inc=1, device_id=peer, device_id_type=MESH)
    pl.semaphore_wait(barrier, len(everyone))

    def send(src, dst, send_sem, recv_sem, peer):
        copy = pltpu.make_async_remote_copy(
            src_ref=src, dst_ref=dst, send_sem=send_sem, recv_sem=recv_sem,
            device_id=peer, device_id_type=MESH,
        )
        copy.start()
        return copy

    everything = []

    def to_x(src, dst, slot, back=False):
        copy = send(src, dst, x_send.at[slot], x_recv.at[slot], x_peers[1 if back else 0])
        everything.append(copy)
        return copy

    def to_y(src, dst, slot, back=False):
        copy = send(src, dst, y_send.at[slot], y_recv.at[slot], y_peers[1 if back else 0])
        everything.append(copy)
        return copy

    to_core = []

    def across(ref):
        slot = len(to_core)
        to_core.append(send(ref, ref, c_send.at[slot], c_recv.at[slot], partner))

    def row(yy):
        return out_ref.at[yy, z, :, core]

    def column(xx):
        return out_ref.at[:, other, xx, core]

    mine = out_ref.at[y, z, x, core]
    own = pltpu.make_async_copy(unit_ref, mine, own_sem)
    own.start()
    to_z = send(unit_ref, mine, z_send, z_recv, z_peer)
    ahead = to_x(unit_ref, mine, 0)
    behind = to_x(unit_ref, mine, 1, True)
    ahead.wait_recv()
    passed = out_ref.at[y, z, x_last, core]
    relay_x = to_x(passed, passed, 2)
    to_z.wait_recv()
    cross = out_ref.at[y, other, x, core]
    up = to_y(cross, cross, 0)
    down = to_y(cross, cross, 1, True)
    own.wait()
    behind.wait_recv()
    relay_x.wait_recv()
    row_up = to_y(row(y), row(y), 3)
    row_down = to_y(row(y), row(y), 4, True)
    across(row(y))
    up.wait_recv()
    passed = out_ref.at[y_last, other, x, core]
    relay_y = to_y(passed, passed, 2)
    down.wait_recv()
    relay_y.wait_recv()
    column_up = to_x(column(x), column(x), 3)
    column_down = to_x(column(x), column(x), 4, True)
    across(column(x))
    row_up.wait_recv()
    row_relay = to_y(row(y_last), row(y_last), 5)
    across(row(y_last))
    row_down.wait_recv()
    across(row(y_next))
    column_up.wait_recv()
    column_relay = to_x(column(x_last), column(x_last), 5)
    across(column(x_last))
    column_down.wait_recv()
    across(column(x_next))
    row_relay.wait_recv()
    across(row(y_far))
    column_relay.wait_recv()
    across(column(x_far))
    for copy in to_core:
        copy.wait_recv()
    for copy in [to_z] + everything + to_core:
        copy.wait_send()


def gather(unit):
    channels, pixels = unit.shape
    dma = pltpu.SemaphoreType.DMA
    out = pl.pallas_call(
        gather_kernel,
        out_shape=jax.ShapeDtypeStruct((NY, NZ, NX, NC, channels, pixels), unit.dtype),
        in_specs=[pl.BlockSpec(memory_space=pl.ANY)],
        out_specs=pl.BlockSpec(memory_space=pl.ANY),
        scratch_shapes=[
            dma,
            dma,
            dma,
            dma((2 * (NX - 1),)),
            dma((2 * (NX - 1),)),
            dma((2 * (NY - 1),)),
            dma((2 * (NY - 1),)),
            dma((NX + NY,)),
            dma((NX + NY,)),
        ],
        compiler_params=pltpu.CompilerParams(
            collective_id=0, has_side_effects=True, vmem_limit_bytes=8 << 20
        ),
    )(unit)
    return out.reshape(NY * NZ * NX * NC, channels, pixels)


def reduce_kernel(
    message_ref, cycles_ref, out_ref, cycles_out_ref,
    got, staged, far,
    own_sem, plane_send, plane_recv, column_send, column_recv, cycle_send, cycle_recv,
):
    dom = lax.axis_index("dom")
    cls = lax.axis_index("cls")
    y = lax.div(dom, NZ * NX)
    z = lax.rem(lax.div(dom, NX), NZ)
    x = lax.rem(dom, NX)
    core = lax.rem(cls, NC)
    groups = far.shape[1]
    rows = far.shape[2]
    doms = NY * NZ * NX

    plane = []
    for dy in range(NY):
        for dx in range(NX):
            plane.append((lax.rem(y + dy, NY), lax.rem(x + dx, NX)))
    column = []
    for dz in range(NZ):
        for dc in range(groups):
            column.append((lax.rem(z + dz, NZ), lax.rem(cls + dc, groups)))
    others = [lax.rem(dom + step, doms) for step in range(1, doms)]

    barrier = pltpu.get_barrier_semaphore()
    greeted = [(there, cls) for there in others]
    for step, (zz, cc) in enumerate(column):
        if step % groups:
            greeted.append(((y * NZ + zz) * NX + x, cc))
    for peer in greeted:
        pl.semaphore_signal(barrier, inc=1, device_id=peer, device_id_type=MESH)
    pl.semaphore_wait(barrier, len(greeted))

    own = pltpu.make_async_copy(message_ref.at[y, :, x], got.at[0], own_sem.at[0])
    own.start()
    own_cycles = pltpu.make_async_copy(cycles_ref, cycles_out_ref.at[dom], own_sem.at[1])
    own_cycles.start()
    sends = []
    for step in range(1, NY * NX):
        yy, xx = plane[step]
        copy = pltpu.make_async_remote_copy(
            src_ref=message_ref.at[yy, :, xx], dst_ref=got.at[step],
            send_sem=plane_send.at[step], recv_sem=plane_recv.at[step],
            device_id=((yy * NZ + z) * NX + xx, cls), device_id_type=MESH,
        )
        copy.start()
        sends.append(copy)
    for there in others:
        pltpu.make_async_remote_copy(
            src_ref=cycles_ref, dst_ref=cycles_out_ref.at[dom],
            send_sem=cycle_send, recv_sem=cycle_recv,
            device_id=(there, cls), device_id_type=MESH,
        ).start()
    own.wait()
    for copy in sends:
        copy.wait_recv()
    for zz in range(NZ):
        total = got[0, zz].astype(jnp.float32)
        for step in range(1, NY * NX):
            total = total + got[step, zz].astype(jnp.float32)
        total = total.astype(jnp.bfloat16)
        for cc in range(NC):
            staged[zz, cc] = total[cc * rows : (cc + 1) * rows]
    kept = pltpu.make_async_copy(staged.at[z, core], far.at[z, cls], own_sem.at[2])
    kept.start()
    relays = []
    for step in range(1, NZ * groups):
        zz, cc = column[step]
        copy = pltpu.make_async_remote_copy(
            src_ref=staged.at[zz, lax.rem(cc, NC)], dst_ref=far.at[z, cls],
            send_sem=column_send.at[step], recv_sem=column_recv.at[step],
            device_id=((y * NZ + zz) * NX + x, cc), device_id_type=MESH,
        )
        copy.start()
        relays.append(copy)
    kept.wait()
    for copy in relays:
        copy.wait_recv()
    for cc in range(groups):
        out_ref[cc] = far[0, cc].astype(jnp.float32) + far[1, cc].astype(jnp.float32)
    own_cycles.wait()
    span = cycles_out_ref.at[pl.ds(0, doms - 1)]
    pltpu.make_async_copy(span, span, cycle_recv).wait()
    pltpu.make_async_copy(span, span, cycle_send).wait()
    for copy in sends + relays:
        copy.wait_send()


def reduce(message, cycles, groups):
    doms, rows, width = message.shape
    dma = pltpu.SemaphoreType.DMA
    half = rows // NC
    return pl.pallas_call(
        reduce_kernel,
        out_shape=(
            jax.ShapeDtypeStruct((groups, half, width), jnp.float32),
            jax.ShapeDtypeStruct((doms,) + cycles.shape, cycles.dtype),
        ),
        in_specs=[pl.BlockSpec(memory_space=pltpu.VMEM)] * 2,
        out_specs=(pl.BlockSpec(memory_space=pltpu.VMEM),) * 2,
        scratch_shapes=[
            pltpu.VMEM((NY * NX, NZ, rows, width), jnp.bfloat16),
            pltpu.VMEM((NZ, NC, half, width), jnp.bfloat16),
            pltpu.VMEM((NZ, groups, half, width), jnp.bfloat16),
            dma((3,)),
            dma((NY * NX,)),
            dma((NY * NX,)),
            dma((NZ * groups,)),
            dma((NZ * groups,)),
            dma,
            dma,
        ],
        compiler_params=pltpu.CompilerParams(
            collective_id=1, has_side_effects=True, vmem_limit_bytes=16 << 20
        ),
    )(message.reshape(NY, NZ, NX, rows, width), cycles)


def split(value):
    parts = []
    for _ in range(3):
        part = lax.reduce_precision(value, 8, 7)
        parts.append(part.astype(jnp.bfloat16))
        value = value - part
    return jnp.concatenate(parts, axis=0)


def local(spectra, classes, halves, groups, cycles, ctf_table, noise):
    local_particles, channels, local_pixels = spectra.shape
    depth = ctf_table.shape[0]
    pixels = ctf_table.shape[1]
    cycle_total = noise.shape[0]
    dom_count = lax.axis_size("dom")
    cls_count = lax.axis_size("cls")
    owned_rows = 2 * K // dom_count
    pixel_begin = lax.axis_index("cls") * local_pixels
    ctf_local = lax.dynamic_slice_in_dim(ctf_table, pixel_begin, local_pixels, 1)
    group_hot = (groups[:, None] == jnp.arange(depth, dtype=jnp.int32)[None, :]).astype(
        jnp.bfloat16
    )
    labels = classes * 2 + halves
    class_hot = (labels[:, None] == jnp.arange(2 * K, dtype=jnp.int32)[None, :]).astype(
        jnp.bfloat16
    )
    ctf = jnp.dot(group_hot, ctf_local, preferred_element_type=jnp.float32)
    weighted = (ctf[:, None, :] * spectra).astype(jnp.bfloat16)
    partial_sums = jnp.einsum("pm,pcn->mcn", class_hot, weighted, preferred_element_type=jnp.float32)
    counts = jnp.einsum("pm,pg->mg", class_hot, group_hot, preferred_element_type=jnp.float32)
    counts = counts.astype(jnp.int32)
    digits = jnp.concatenate(
        [counts % STEP, (counts // STEP) % STEP, counts // (STEP * STEP)], axis=1
    )
    spare = -(local_pixels + 3 * depth) % LANES + 3 * depth
    digits = jnp.pad(digits[:, None, :], ((0, 0), (0, channels - 1), (0, spare - 3 * depth)))
    message = jnp.concatenate(
        [partial_sums.astype(jnp.bfloat16), digits.astype(jnp.bfloat16)], axis=2
    )
    cycle_rows = -(-cycles.shape[0] // (8 * LANES)) * 8
    cycle_block = jnp.pad(cycles, (0, cycle_rows * LANES - cycles.shape[0]))
    incoming, every_cycle = reduce(
        message.reshape(dom_count, owned_rows * channels, local_pixels + spare),
        cycle_block.reshape(cycle_rows, LANES),
        cls_count,
    )
    every_cycle = every_cycle.reshape(dom_count, -1)[:, : cycles.shape[0]].reshape(pixels)
    sums = jnp.transpose(incoming[:, :, :local_pixels], (1, 0, 2)).reshape(2, channels, pixels)
    found = incoming[0, ::channels, local_pixels : local_pixels + 3 * depth].reshape(2, 3, depth)
    count_mine = found[:, 0] + STEP * found[:, 1] + (STEP * STEP) * found[:, 2]
    square_table = (ctf_table.astype(jnp.float32) ** 2).astype(jnp.bfloat16)
    parts = jnp.dot(split(count_mine), square_table, preferred_element_type=jnp.float32)
    wsum = parts.reshape(3, 2, pixels).sum(axis=0)
    halfavg = sums / (wsum[:, None, :] + RIDGE)
    merged = (sums[0] + sums[1]) / (wsum[0] + wsum[1] + RIDGE)[None, :]
    statistics = jnp.stack(
        [
            jnp.sum(halfavg[0] * halfavg[1], axis=0),
            jnp.sum(halfavg[0] * halfavg[0], axis=0),
            jnp.sum(halfavg[1] * halfavg[1], axis=0),
            jnp.sum(merged * merged, axis=0),
        ],
        axis=0,
    )
    rings = jnp.arange(cycle_total, dtype=jnp.int32)
    cycle_hot = (rings[:, None] == every_cycle[None, :]).astype(jnp.bfloat16)
    totals = jnp.einsum("sn,rn->sr", split(statistics), cycle_hot, preferred_element_type=jnp.float32)
    totals = totals.reshape(3, 4, cycle_total).sum(axis=0)
    correlation = totals[0] / jnp.sqrt((totals[1] + noise) * (totals[2] + noise))
    gain = jnp.maximum(correlation, GAIN_FLOOR)
    power_mean = jnp.sum(gain * gain * totals[3]) / (2.0 * pixels)
    scale = (gain / jnp.sqrt(power_mean + EPSILON))[None, :]
    scale_pixels = jnp.sum(
        jnp.dot(split(scale), cycle_hot, preferred_element_type=jnp.float32), axis=0
    )
    return gather((merged * scale_pixels[None, :]).astype(jnp.bfloat16))


def solution(mesh):
    placed = (P("dom", None, "cls"), P("dom"), P("dom"), P("dom"), P("dom"), P(), P())
    return jax.shard_map(local, mesh=mesh, in_specs=placed, out_specs=P(), check_vma=False)
```

```python
import functools

import jax
import jax.numpy as jnp
from jax import lax
from jax.experimental import pallas as pl
from jax.experimental.pallas import tpu as pltpu
from jax.sharding import PartitionSpec as P

K = 64
RIDGE = 1.0
GAIN_FLOOR = 0.02
EPSILON = 1e-06
STEP = 16
LANES = 128
NY, NZ, NX, NC = 4, 2, 4, 2
MESH = pl.DeviceIdType.MESH


def gather_kernel(unit_ref, out_ref, own_sem, z_send, z_recv, x_send, x_recv, y_send, y_recv, c_send, c_recv):
    dom = lax.axis_index("dom")
    cls = lax.axis_index("cls")
    y = lax.div(dom, NZ * NX)
    z = lax.rem(lax.div(dom, NX), NZ)
    x = lax.rem(dom, NX)
    core = lax.rem(cls, NC)
    other = 1 - z

    def at(yy, zz, xx):
        return ((yy * NZ + zz) * NX + xx, cls)

    partner = (dom, cls + 1 - 2 * core)
    mirrored = lax.axis_size("cls") - NC - (cls - core) + core
    z_peer = (at(y, other, x)[0], mirrored)
    turn = 1 - 2 * core
    x_next, x_last = lax.rem(x + turn + NX, NX), lax.rem(x - turn + NX, NX)
    y_next, y_last = lax.rem(y + turn + NY, NY), lax.rem(y - turn + NY, NY)
    x_far, y_far = lax.rem(x + 2, NX), lax.rem(y + 2, NY)
    x_peers = [at(y, z, x_next), at(y, z, x_last)]
    y_peers = [at(y_next, z, x), at(y_last, z, x)]
    x_partner = (at(y, z, x_last)[0], partner[1])
    y_partner = (at(y_last, z, x)[0], partner[1])

    barrier = pltpu.get_barrier_semaphore()
    everyone = [partner, z_peer, x_partner, y_partner] + x_peers + y_peers
    for peer in everyone:
        pl.semaphore_signal(barrier, inc=1, device_id=peer, device_id_type=MESH)
    pl.semaphore_wait(barrier, len(everyone))

    def send(src, dst, send_sem, recv_sem, peer):
        copy = pltpu.make_async_remote_copy(
            src_ref=src, dst_ref=dst, send_sem=send_sem, recv_sem=recv_sem,
            device_id=peer, device_id_type=MESH,
        )
        copy.start()
        return copy

    everything = []

    def to_x(src, dst, slot, back=False):
        copy = send(src, dst, x_send.at[slot], x_recv.at[slot], x_peers[1 if back else 0])
        everything.append(copy)
        return copy

    def to_y(src, dst, slot, back=False):
        copy = send(src, dst, y_send.at[slot], y_recv.at[slot], y_peers[1 if back else 0])
        everything.append(copy)
        return copy

    to_core = []

    def across(ref, peer=partner):
        slot = len(to_core)
        to_core.append(send(ref, ref, c_send.at[slot], c_recv.at[slot], peer))

    def row(yy):
        return out_ref.at[yy, z, :, core]

    def column(xx):
        return out_ref.at[:, other, xx, core]

    mine = out_ref.at[y, z, x, core]
    own = pltpu.make_async_copy(unit_ref, mine, own_sem)
    own.start()
    to_z = send(unit_ref, mine, z_send, z_recv, z_peer)
    ahead = to_x(unit_ref, mine, 0)
    behind = to_x(unit_ref, mine, 1, True)
    ahead.wait_recv()
    passed = out_ref.at[y, z, x_last, core]
    relay_x = to_x(passed, passed, 2)
    to_z.wait_recv()
    cross = out_ref.at[y, other, x, core]
    up = to_y(cross, cross, 0)
    down = to_y(cross, cross, 1, True)
    own.wait()
    behind.wait_recv()
    relay_x.wait_recv()
    row_up = to_y(row(y), row(y), 3)
    row_down = to_y(row(y), row(y), 4, True)
    across(row(y))
    across(row(y), y_partner)
    up.wait_recv()
    passed = out_ref.at[y_last, other, x, core]
    relay_y = to_y(passed, passed, 2)
    down.wait_recv()
    relay_y.wait_recv()
    column_up = to_x(column(x), column(x), 3)
    column_down = to_x(column(x), column(x), 4, True)
    across(column(x))
    across(column(x), x_partner)
    row_up.wait_recv()
    row_relay = to_y(row(y_last), row(y_last), 5)
    across(row(y_last))
    row_down.wait_recv()
    column_up.wait_recv()
    column_relay = to_x(column(x_last), column(x_last), 5)
    across(column(x_last))
    column_down.wait_recv()
    row_relay.wait_recv()
    across(row(y_far))
    column_relay.wait_recv()
    across(column(x_far))
    for copy in to_core:
        copy.wait_recv()
    for copy in [to_z] + everything + to_core:
        copy.wait_send()


def gather(unit):
    channels, pixels = unit.shape
    dma = pltpu.SemaphoreType.DMA
    out = pl.pallas_call(
        gather_kernel,
        out_shape=jax.ShapeDtypeStruct((NY, NZ, NX, NC, channels, pixels), unit.dtype),
        in_specs=[pl.BlockSpec(memory_space=pl.ANY)],
        out_specs=pl.BlockSpec(memory_space=pl.ANY),
        scratch_shapes=[
            dma,
            dma,
            dma,
            dma((2 * (NX - 1),)),
            dma((2 * (NX - 1),)),
            dma((2 * (NY - 1),)),
            dma((2 * (NY - 1),)),
            dma((NX + NY,)),
            dma((NX + NY,)),
        ],
        compiler_params=pltpu.CompilerParams(
            collective_id=0, has_side_effects=True, vmem_limit_bytes=8 << 20
        ),
    )(unit)
    return out.reshape(NY * NZ * NX * NC, channels, pixels)


def reduce_kernel(
    message_ref, cycles_ref, out_ref, cycles_out_ref,
    got, staged, far,
    own_sem, plane_send, plane_recv, column_send, column_recv, cycle_send, cycle_recv,
):
    dom = lax.axis_index("dom")
    cls = lax.axis_index("cls")
    y = lax.div(dom, NZ * NX)
    z = lax.rem(lax.div(dom, NX), NZ)
    x = lax.rem(dom, NX)
    core = lax.rem(cls, NC)
    groups = far.shape[1]
    rows = far.shape[2]
    doms = NY * NZ * NX

    plane = []
    for dy in range(NY):
        for dx in range(NX):
            plane.append((lax.rem(y + dy, NY), lax.rem(x + dx, NX)))
    column = []
    for dz in range(NZ):
        for dc in range(groups):
            column.append((lax.rem(z + dz, NZ), lax.rem(cls + dc, groups)))
    others = [lax.rem(dom + step, doms) for step in range(1, doms)]

    barrier = pltpu.get_barrier_semaphore()
    greeted = [(there, cls) for there in others]
    for step, (zz, cc) in enumerate(column):
        if step % groups:
            greeted.append(((y * NZ + zz) * NX + x, cc))
    for peer in greeted:
        pl.semaphore_signal(barrier, inc=1, device_id=peer, device_id_type=MESH)
    pl.semaphore_wait(barrier, len(greeted))

    own = pltpu.make_async_copy(message_ref.at[y, :, x], got.at[0], own_sem.at[0])
    own.start()
    own_cycles = pltpu.make_async_copy(cycles_ref, cycles_out_ref.at[dom], own_sem.at[1])
    own_cycles.start()
    sends = []
    for step in range(1, NY * NX):
        yy, xx = plane[step]
        copy = pltpu.make_async_remote_copy(
            src_ref=message_ref.at[yy, :, xx], dst_ref=got.at[step],
            send_sem=plane_send.at[step], recv_sem=plane_recv.at[step],
            device_id=((yy * NZ + z) * NX + xx, cls), device_id_type=MESH,
        )
        copy.start()
        sends.append(copy)
    for there in others:
        pltpu.make_async_remote_copy(
            src_ref=cycles_ref, dst_ref=cycles_out_ref.at[dom],
            send_sem=cycle_send, recv_sem=cycle_recv,
            device_id=(there, cls), device_id_type=MESH,
        ).start()
    own.wait()
    for copy in sends:
        copy.wait_recv()
    for zz in range(NZ):
        total = got[0, zz].astype(jnp.float32)
        for step in range(1, NY * NX):
            total = total + got[step, zz].astype(jnp.float32)
        total = total.astype(jnp.bfloat16)
        for cc in range(NC):
            staged[zz, cc] = total[cc * rows : (cc + 1) * rows]
    kept = pltpu.make_async_copy(staged.at[z, core], far.at[z, cls], own_sem.at[2])
    kept.start()
    relays = []
    for step in range(1, NZ * groups):
        zz, cc = column[step]
        copy = pltpu.make_async_remote_copy(
            src_ref=staged.at[zz, lax.rem(cc, NC)], dst_ref=far.at[z, cls],
            send_sem=column_send.at[step], recv_sem=column_recv.at[step],
            device_id=((y * NZ + zz) * NX + x, cc), device_id_type=MESH,
        )
        copy.start()
        relays.append(copy)
    kept.wait()
    for copy in relays:
        copy.wait_recv()
    for cc in range(groups):
        out_ref[cc] = far[0, cc].astype(jnp.float32) + far[1, cc].astype(jnp.float32)
    own_cycles.wait()
    span = cycles_out_ref.at[pl.ds(0, doms - 1)]
    pltpu.make_async_copy(span, span, cycle_recv).wait()
    pltpu.make_async_copy(span, span, cycle_send).wait()
    for copy in sends + relays:
        copy.wait_send()


def reduce(message, cycles, groups):
    doms, rows, width = message.shape
    dma = pltpu.SemaphoreType.DMA
    half = rows // NC
    return pl.pallas_call(
        reduce_kernel,
        out_shape=(
            jax.ShapeDtypeStruct((groups, half, width), jnp.float32),
            jax.ShapeDtypeStruct((doms,) + cycles.shape, cycles.dtype),
        ),
        in_specs=[pl.BlockSpec(memory_space=pltpu.VMEM)] * 2,
        out_specs=(pl.BlockSpec(memory_space=pltpu.VMEM),) * 2,
        scratch_shapes=[
            pltpu.VMEM((NY * NX, NZ, rows, width), jnp.bfloat16),
            pltpu.VMEM((NZ, NC, half, width), jnp.bfloat16),
            pltpu.VMEM((NZ, groups, half, width), jnp.bfloat16),
            dma((3,)),
            dma((NY * NX,)),
            dma((NY * NX,)),
            dma((NZ * groups,)),
            dma((NZ * groups,)),
            dma,
            dma,
        ],
        compiler_params=pltpu.CompilerParams(
            collective_id=1, has_side_effects=True, vmem_limit_bytes=16 << 20
        ),
    )(message.reshape(NY, NZ, NX, rows, width), cycles)


def split(value):
    parts = []
    for _ in range(3):
        part = lax.reduce_precision(value, 8, 7)
        parts.append(part.astype(jnp.bfloat16))
        value = value - part
    return jnp.concatenate(parts, axis=0)


def local(spectra, classes, halves, groups, cycles, ctf_table, noise):
    local_particles, channels, local_pixels = spectra.shape
    depth = ctf_table.shape[0]
    pixels = ctf_table.shape[1]
    cycle_total = noise.shape[0]
    dom_count = lax.axis_size("dom")
    cls_count = lax.axis_size("cls")
    owned_rows = 2 * K // dom_count
    pixel_begin = lax.axis_index("cls") * local_pixels
    ctf_local = lax.dynamic_slice_in_dim(ctf_table, pixel_begin, local_pixels, 1)
    group_hot = (groups[:, None] == jnp.arange(depth, dtype=jnp.int32)[None, :]).astype(
        jnp.bfloat16
    )
    labels = classes * 2 + halves
    class_hot = (labels[:, None] == jnp.arange(2 * K, dtype=jnp.int32)[None, :]).astype(
        jnp.bfloat16
    )
    ctf = jnp.dot(group_hot, ctf_local, preferred_element_type=jnp.float32)
    weighted = (ctf[:, None, :] * spectra).astype(jnp.bfloat16)
    partial_sums = jnp.einsum("pm,pcn->mcn", class_hot, weighted, preferred_element_type=jnp.float32)
    counts = jnp.einsum("pm,pg->mg", class_hot, group_hot, preferred_element_type=jnp.float32)
    counts = counts.astype(jnp.int32)
    digits = jnp.concatenate(
        [counts % STEP, (counts // STEP) % STEP, counts // (STEP * STEP)], axis=1
    )
    spare = -(local_pixels + 3 * depth) % LANES + 3 * depth
    digits = jnp.pad(digits[:, None, :], ((0, 0), (0, channels - 1), (0, spare - 3 * depth)))
    message = jnp.concatenate(
        [partial_sums.astype(jnp.bfloat16), digits.astype(jnp.bfloat16)], axis=2
    )
    cycle_rows = -(-cycles.shape[0] // (8 * LANES)) * 8
    cycle_block = jnp.pad(cycles, (0, cycle_rows * LANES - cycles.shape[0]))
    incoming, every_cycle = reduce(
        message.reshape(dom_count, owned_rows * channels, local_pixels + spare),
        cycle_block.reshape(cycle_rows, LANES),
        cls_count,
    )
    every_cycle = every_cycle.reshape(dom_count, -1)[:, : cycles.shape[0]].reshape(pixels)
    sums = jnp.transpose(incoming[:, :, :local_pixels], (1, 0, 2)).reshape(2, channels, pixels)
    found = incoming[0, ::channels, local_pixels : local_pixels + 3 * depth].reshape(2, 3, depth)
    count_mine = found[:, 0] + STEP * found[:, 1] + (STEP * STEP) * found[:, 2]
    square_table = (ctf_table.astype(jnp.float32) ** 2).astype(jnp.bfloat16)
    parts = jnp.dot(split(count_mine), square_table, preferred_element_type=jnp.float32)
    wsum = parts.reshape(3, 2, pixels).sum(axis=0)
    halfavg = sums / (wsum[:, None, :] + RIDGE)
    merged = (sums[0] + sums[1]) / (wsum[0] + wsum[1] + RIDGE)[None, :]
    statistics = jnp.stack(
        [
            jnp.sum(halfavg[0] * halfavg[1], axis=0),
            jnp.sum(halfavg[0] * halfavg[0], axis=0),
            jnp.sum(halfavg[1] * halfavg[1], axis=0),
            jnp.sum(merged * merged, axis=0),
        ],
        axis=0,
    )
    rings = jnp.arange(cycle_total, dtype=jnp.int32)
    cycle_hot = (rings[:, None] == every_cycle[None, :]).astype(jnp.bfloat16)
    totals = jnp.einsum("sn,rn->sr", split(statistics), cycle_hot, preferred_element_type=jnp.float32)
    totals = totals.reshape(3, 4, cycle_total).sum(axis=0)
    correlation = totals[0] / jnp.sqrt((totals[1] + noise) * (totals[2] + noise))
    gain = jnp.maximum(correlation, GAIN_FLOOR)
    power_mean = jnp.sum(gain * gain * totals[3]) / (2.0 * pixels)
    scale = (gain / jnp.sqrt(power_mean + EPSILON))[None, :]
    scale_pixels = jnp.sum(
        jnp.dot(split(scale), cycle_hot, preferred_element_type=jnp.float32), axis=0
    )
    return gather((merged * scale_pixels[None, :]).astype(jnp.bfloat16))


def solution(mesh):
    placed = (P("dom", None, "cls"), P("dom"), P("dom"), P("dom"), P("dom"), P(), P())
    return jax.shard_map(local, mesh=mesh, in_specs=placed, out_specs=P(), check_vma=False)
```

```python
import functools

import jax
import jax.numpy as jnp
from jax import lax
from jax.experimental import pallas as pl
from jax.experimental.pallas import tpu as pltpu
from jax.sharding import PartitionSpec as P

K = 64
RIDGE = 1.0
GAIN_FLOOR = 0.02
EPSILON = 1e-06
STEP = 16
LANES = 128
NY, NZ, NX, NC = 4, 2, 4, 2
MESH = pl.DeviceIdType.MESH


def gather_kernel(unit_ref, out_ref, own_sem, z_send, z_recv, x_send, x_recv, y_send, y_recv, c_send, c_recv):
    dom = lax.axis_index("dom")
    cls = lax.axis_index("cls")
    y = lax.div(dom, NZ * NX)
    z = lax.rem(lax.div(dom, NX), NZ)
    x = lax.rem(dom, NX)
    core = lax.rem(cls, NC)
    other = 1 - z

    def at(yy, zz, xx):
        return ((yy * NZ + zz) * NX + xx, cls)

    partner = (dom, cls + 1 - 2 * core)
    mirrored = lax.axis_size("cls") - NC - (cls - core) + core
    z_peer = (at(y, other, x)[0], mirrored)
    x_peers = [at(y, z, lax.rem(x + j, NX)) for j in range(1, NX)]
    y_peers = [at(lax.rem(y + j, NY), z, x) for j in range(1, NY)]
    x_from = [lax.rem(x + NX - j, NX) for j in range(1, NX)]
    y_from = [lax.rem(y + NY - j, NY) for j in range(1, NY)]

    barrier = pltpu.get_barrier_semaphore()
    everyone = [partner, z_peer] + x_peers + y_peers
    for peer in everyone:
        pl.semaphore_signal(barrier, inc=1, device_id=peer, device_id_type=MESH)
    pl.semaphore_wait(barrier, len(everyone))

    def send(src, dst, send_sem, recv_sem, peer):
        copy = pltpu.make_async_remote_copy(
            src_ref=src, dst_ref=dst, send_sem=send_sem, recv_sem=recv_sem,
            device_id=peer, device_id_type=MESH,
        )
        copy.start()
        return copy

    mine = out_ref.at[y, z, x, core]
    own = pltpu.make_async_copy(unit_ref, mine, own_sem)
    own.start()
    to_z = send(unit_ref, mine, z_send, z_recv, z_peer)
    first_x = [
        send(unit_ref, mine, x_send.at[j], x_recv.at[j], x_peers[j]) for j in range(NX - 1)
    ]
    to_z.wait_recv()
    cross = out_ref.at[y, other, x, core]
    first_y = [send(cross, cross, y_send.at[j], y_recv.at[j], y_peers[j]) for j in range(NY - 1)]
    own.wait()
    for copy in first_x:
        copy.wait_recv()
    row = out_ref.at[y, z, :, core]
    second_y = [
        send(row, row, y_send.at[NY - 1 + j], y_recv.at[NY - 1 + j], y_peers[j])
        for j in range(NY - 1)
    ]
    to_core = [send(row, row, c_send.at[0], c_recv.at[0], partner)]
    for copy in first_y:
        copy.wait_recv()
    column = out_ref.at[:, other, x, core]
    second_x = [
        send(column, column, x_send.at[NX - 1 + j], x_recv.at[NX - 1 + j], x_peers[j])
        for j in range(NX - 1)
    ]
    to_core.append(send(column, column, c_send.at[1], c_recv.at[1], partner))
    for j in range(NY - 1):
        second_y[j].wait_recv()
        far = out_ref.at[y_from[j], z, :, core]
        to_core.append(send(far, far, c_send.at[2 + j], c_recv.at[2 + j], partner))
    for j in range(NX - 1):
        second_x[j].wait_recv()
        far = out_ref.at[:, other, x_from[j], core]
        slot = 1 + NY + j
        to_core.append(send(far, far, c_send.at[slot], c_recv.at[slot], partner))
    for copy in to_core:
        copy.wait_recv()
    for copy in [to_z] + first_x + first_y + second_y + second_x + to_core:
        copy.wait_send()


def gather(unit):
    channels, pixels = unit.shape
    dma = pltpu.SemaphoreType.DMA
    out = pl.pallas_call(
        gather_kernel,
        out_shape=jax.ShapeDtypeStruct((NY, NZ, NX, NC, channels, pixels), unit.dtype),
        in_specs=[pl.BlockSpec(memory_space=pl.ANY)],
        out_specs=pl.BlockSpec(memory_space=pl.ANY),
        scratch_shapes=[
            dma,
            dma,
            dma,
            dma((2 * (NX - 1),)),
            dma((2 * (NX - 1),)),
            dma((2 * (NY - 1),)),
            dma((2 * (NY - 1),)),
            dma((NX + NY,)),
            dma((NX + NY,)),
        ],
        compiler_params=pltpu.CompilerParams(
            collective_id=0, has_side_effects=True, vmem_limit_bytes=8 << 20
        ),
    )(unit)
    return out.reshape(NY * NZ * NX * NC, channels, pixels)


def reduce_kernel(
    message_ref, cycles_ref, out_ref, cycles_out_ref,
    got, staged, far,
    own_sem, plane_send, plane_recv, column_send, column_recv, cycle_send, cycle_recv,
):
    dom = lax.axis_index("dom")
    cls = lax.axis_index("cls")
    y = lax.div(dom, NZ * NX)
    z = lax.rem(lax.div(dom, NX), NZ)
    x = lax.rem(dom, NX)
    core = lax.rem(cls, NC)
    groups = far.shape[1]
    rows = far.shape[2]
    doms = NY * NZ * NX

    plane = []
    for dy in range(NY):
        for dx in range(NX):
            plane.append((lax.rem(y + dy, NY), lax.rem(x + dx, NX)))
    column = []
    for dz in range(NZ):
        for dc in range(groups):
            column.append((lax.rem(z + dz, NZ), lax.rem(cls + dc, groups)))
    others = [lax.rem(dom + step, doms) for step in range(1, doms)]

    barrier = pltpu.get_barrier_semaphore()
    greeted = [(there, cls) for there in others]
    for step, (zz, cc) in enumerate(column):
        if step % groups:
            greeted.append(((y * NZ + zz) * NX + x, cc))
    for peer in greeted:
        pl.semaphore_signal(barrier, inc=1, device_id=peer, device_id_type=MESH)
    pl.semaphore_wait(barrier, len(greeted))

    own = pltpu.make_async_copy(message_ref.at[y, :, x], got.at[0], own_sem.at[0])
    own.start()
    own_cycles = pltpu.make_async_copy(cycles_ref, cycles_out_ref.at[dom], own_sem.at[1])
    own_cycles.start()
    sends = []
    far_first = sorted(
        range(1, NY * NX), key=lambda step: -(step // NX == NY // 2) - (step % NX == NX // 2)
    )
    for step in far_first:
        yy, xx = plane[step]
        copy = pltpu.make_async_remote_copy(
            src_ref=message_ref.at[yy, :, xx], dst_ref=got.at[step],
            send_sem=plane_send.at[step], recv_sem=plane_recv.at[step],
            device_id=((yy * NZ + z) * NX + xx, cls), device_id_type=MESH,
        )
        copy.start()
        sends.append(copy)
    for there in others:
        pltpu.make_async_remote_copy(
            src_ref=cycles_ref, dst_ref=cycles_out_ref.at[dom],
            send_sem=cycle_send, recv_sem=cycle_recv,
            device_id=(there, cls), device_id_type=MESH,
        ).start()
    own.wait()
    for copy in sends:
        copy.wait_recv()
    for zz in range(NZ):
        total = got[0, zz].astype(jnp.float32)
        for step in range(1, NY * NX):
            total = total + got[step, zz].astype(jnp.float32)
        total = total.astype(jnp.bfloat16)
        for cc in range(NC):
            staged[zz, cc] = total[cc * rows : (cc + 1) * rows]
    kept = pltpu.make_async_copy(staged.at[z, core], far.at[z, cls], own_sem.at[2])
    kept.start()
    relays = []
    for step in range(1, NZ * groups):
        zz, cc = column[step]
        copy = pltpu.make_async_remote_copy(
            src_ref=staged.at[zz, lax.rem(cc, NC)], dst_ref=far.at[z, cls],
            send_sem=column_send.at[step], recv_sem=column_recv.at[step],
            device_id=((y * NZ + zz) * NX + x, cc), device_id_type=MESH,
        )
        copy.start()
        relays.append(copy)
    kept.wait()
    for copy in relays:
        copy.wait_recv()
    for cc in range(groups):
        out_ref[cc] = far[0, cc].astype(jnp.float32) + far[1, cc].astype(jnp.float32)
    own_cycles.wait()
    span = cycles_out_ref.at[pl.ds(0, doms - 1)]
    pltpu.make_async_copy(span, span, cycle_recv).wait()
    pltpu.make_async_copy(span, span, cycle_send).wait()
    for copy in sends + relays:
        copy.wait_send()


def reduce(message, cycles, groups):
    doms, rows, width = message.shape
    dma = pltpu.SemaphoreType.DMA
    half = rows // NC
    return pl.pallas_call(
        reduce_kernel,
        out_shape=(
            jax.ShapeDtypeStruct((groups, half, width), jnp.float32),
            jax.ShapeDtypeStruct((doms,) + cycles.shape, cycles.dtype),
        ),
        in_specs=[pl.BlockSpec(memory_space=pltpu.VMEM)] * 2,
        out_specs=(pl.BlockSpec(memory_space=pltpu.VMEM),) * 2,
        scratch_shapes=[
            pltpu.VMEM((NY * NX, NZ, rows, width), jnp.bfloat16),
            pltpu.VMEM((NZ, NC, half, width), jnp.bfloat16),
            pltpu.VMEM((NZ, groups, half, width), jnp.bfloat16),
            dma((3,)),
            dma((NY * NX,)),
            dma((NY * NX,)),
            dma((NZ * groups,)),
            dma((NZ * groups,)),
            dma,
            dma,
        ],
        compiler_params=pltpu.CompilerParams(
            collective_id=1, has_side_effects=True, vmem_limit_bytes=16 << 20
        ),
    )(message.reshape(NY, NZ, NX, rows, width), cycles)


def split(value):
    parts = []
    for _ in range(3):
        part = lax.reduce_precision(value, 8, 7)
        parts.append(part.astype(jnp.bfloat16))
        value = value - part
    return jnp.concatenate(parts, axis=0)


def local(spectra, classes, halves, groups, cycles, ctf_table, noise):
    local_particles, channels, local_pixels = spectra.shape
    depth = ctf_table.shape[0]
    pixels = ctf_table.shape[1]
    cycle_total = noise.shape[0]
    dom_count = lax.axis_size("dom")
    cls_count = lax.axis_size("cls")
    owned_rows = 2 * K // dom_count
    pixel_begin = lax.axis_index("cls") * local_pixels
    ctf_local = lax.dynamic_slice_in_dim(ctf_table, pixel_begin, local_pixels, 1)
    group_hot = (groups[:, None] == jnp.arange(depth, dtype=jnp.int32)[None, :]).astype(
        jnp.bfloat16
    )
    labels = classes * 2 + halves
    class_hot = (labels[:, None] == jnp.arange(2 * K, dtype=jnp.int32)[None, :]).astype(
        jnp.bfloat16
    )
    ctf = jnp.dot(group_hot, ctf_local, preferred_element_type=jnp.float32)
    weighted = (ctf[:, None, :] * spectra).astype(jnp.bfloat16)
    partial_sums = jnp.einsum("pm,pcn->mcn", class_hot, weighted, preferred_element_type=jnp.float32)
    counts = jnp.einsum("pm,pg->mg", class_hot, group_hot, preferred_element_type=jnp.float32)
    counts = counts.astype(jnp.int32)
    digits = jnp.concatenate(
        [counts % STEP, (counts // STEP) % STEP, counts // (STEP * STEP)], axis=1
    )
    spare = -(local_pixels + 3 * depth) % LANES + 3 * depth
    digits = jnp.pad(digits[:, None, :], ((0, 0), (0, channels - 1), (0, spare - 3 * depth)))
    message = jnp.concatenate(
        [partial_sums.astype(jnp.bfloat16), digits.astype(jnp.bfloat16)], axis=2
    )
    cycle_rows = -(-cycles.shape[0] // (8 * LANES)) * 8
    cycle_block = jnp.pad(cycles, (0, cycle_rows * LANES - cycles.shape[0]))
    incoming, every_cycle = reduce(
        message.reshape(dom_count, owned_rows * channels, local_pixels + spare),
        cycle_block.reshape(cycle_rows, LANES),
        cls_count,
    )
    every_cycle = every_cycle.reshape(dom_count, -1)[:, : cycles.shape[0]].reshape(pixels)
    sums = jnp.transpose(incoming[:, :, :local_pixels], (1, 0, 2)).reshape(2, channels, pixels)
    found = incoming[0, ::channels, local_pixels : local_pixels + 3 * depth].reshape(2, 3, depth)
    count_mine = found[:, 0] + STEP * found[:, 1] + (STEP * STEP) * found[:, 2]
    square_table = (ctf_table.astype(jnp.float32) ** 2).astype(jnp.bfloat16)
    parts = jnp.dot(split(count_mine), square_table, preferred_element_type=jnp.float32)
    wsum = parts.reshape(3, 2, pixels).sum(axis=0)
    halfavg = sums / (wsum[:, None, :] + RIDGE)
    merged = (sums[0] + sums[1]) / (wsum[0] + wsum[1] + RIDGE)[None, :]
    statistics = jnp.stack(
        [
            jnp.sum(halfavg[0] * halfavg[1], axis=0),
            jnp.sum(halfavg[0] * halfavg[0], axis=0),
            jnp.sum(halfavg[1] * halfavg[1], axis=0),
            jnp.sum(merged * merged, axis=0),
        ],
        axis=0,
    )
    rings = jnp.arange(cycle_total, dtype=jnp.int32)
    cycle_hot = (rings[:, None] == every_cycle[None, :]).astype(jnp.bfloat16)
    totals = jnp.einsum("sn,rn->sr", split(statistics), cycle_hot, preferred_element_type=jnp.float32)
    totals = totals.reshape(3, 4, cycle_total).sum(axis=0)
    correlation = totals[0] / jnp.sqrt((totals[1] + noise) * (totals[2] + noise))
    gain = jnp.maximum(correlation, GAIN_FLOOR)
    power_mean = jnp.sum(gain * gain * totals[3]) / (2.0 * pixels)
    scale = (gain / jnp.sqrt(power_mean + EPSILON))[None, :]
    scale_pixels = jnp.sum(
        jnp.dot(split(scale), cycle_hot, preferred_element_type=jnp.float32), axis=0
    )
    return gather((merged * scale_pixels[None, :]).astype(jnp.bfloat16))


def solution(mesh):
    placed = (P("dom", None, "cls"), P("dom"), P("dom"), P("dom"), P("dom"), P(), P())
    return jax.shard_map(local, mesh=mesh, in_specs=placed, out_specs=P(), check_vma=False)
```
